256 devices in a mesh: section: 8 (over y, core), seq: 32 (over x, z).
Axes of the slice: x: 4, y: 4, z: 8, core: 2. Of those that a mesh axis runs over, the one named last changes fastest.
Arguments:
- activations: bfloat16 [8, 16384, 2048], P('section', 'seq'), may hold values from -6 to 6
- norm_gain: float32 [8, 2048], P('section'), may hold values from 0.5 to 1.5
- value_weight: bfloat16 [8, 2048, 1024], P('section'), may hold values from -0.125 to 0.125
- shared_weight: bfloat16 [8, 2048, 256], P('section'), may hold values from -0.125 to 0.125
- rate_weight: bfloat16 [8, 2048, 8], P('section'), may hold values from -0.125 to 0.125
- rate_bias: float32 [8, 8], P('section'), may hold values from -1 to 1
- decay_rate: float32 [8, 8], P('section'), may hold values from 3.0517578e-05 to 0.03
- level_table: float32 [8, 16, 15, 8], P('section'), may hold values from 0.25 to 2
- level_ids: int32 [8, 16384, 15], P('section', 'seq'), may hold values from 0 to 15
- out_gain: float32 [8, 1024], P('section'), may hold values from 0.5 to 1.5
- out_weight: bfloat16 [8, 1024, 2048], P('section'), may hold values from -0.1875 to 0.1875
Outputs:
- result: bfloat16 [8, 16384, 2048], P('section', 'seq')
The draws below stay inside these ranges and needn't reach their ends.
All inputs are finite; a program needn't handle non-finite values.
Results may differ from the reference program's by a relative error of at most 0.03.
Values may be sent and summed in bfloat16 or wider, within the bound.
No kernel may reach another device: no remote copies, remote signals or barrier semaphores. Data moves between devices by JAX's collectives and lax.ppermute only.
A program may use at most 128 MiB of HBM per device.

```python
import math
import jax
import jax.numpy as jnp
from jax import lax

D = 2048
HW = 8
P_SIZE = 128
N = 128
BUCKETS = 16
TOK_DEV = 512
TOK_BITS = 9
SEQ_BITS = 5
LEVELS = 15
TOKENS = 16384
SECTIONS = 8
N_SEQ = 32


def with_ends(array, stream_key, smallest, high):
    longest = array.shape.index(max(array.shape))
    spots = []
    for shift in (0, 1):
        where = [jax.random.randint(jax.random.fold_in(stream_key, axis), (), 0, length) for axis, length in enumerate(array.shape)]
        where[longest] = (where[longest] + shift) % array.shape[longest]
        spots.append(tuple(where))
    return array.at[spots[0]].set(smallest).at[spots[1]].set(high)


def level_of(rng, dims, split, smallest, largest):
    def one(dim, shards_of):
        draws = jax.random.uniform(jax.random.fold_in(jax.random.fold_in(rng, 6), dim), (shards_of,), jnp.float32, smallest / len(split), largest / len(split))
        return jnp.repeat(jnp.exp(draws), dims[dim] // shards_of).reshape((-1,) + (1,) * (len(dims) - dim - 1))

    gain = one(*split[0])
    for cut in split[1:]:
        gain = gain * one(*cut)
    return gain


def centred(key, extent, deviation, bound, shards=(), kind=jnp.bfloat16):
    loudness = level_of(key, extent, shards, -0.22, 0.18) if shards else 1.0
    values = jax.random.normal(key, extent, jnp.float32) * deviation * loudness
    return jnp.minimum(jnp.maximum(values, -bound), bound).astype(kind)


def setup_inputs(seed: int = 0) -> dict:
    streams_of = jax.random.split(jax.random.key(seed), 12)
    return {
        "activations": centred(streams_of[0], (SECTIONS, TOKENS, D), 1.0, 6.0, ((0, 8), (1, 32))),
        "norm_gain": jnp.clip(1.0 + 0.1 * jax.random.normal(streams_of[1], (SECTIONS, D), jnp.float32), 0.5, 1.5),
        "value_weight": centred(streams_of[2], (SECTIONS, D, HW * P_SIZE), D ** -0.5, 0.125, ((0, 8),)),
        "shared_weight": centred(streams_of[3], (SECTIONS, D, 2 * N), D ** -0.5, 0.125, ((0, 8),)),
        "rate_weight": centred(streams_of[4], (SECTIONS, D, HW), D ** -0.5, 0.125, ((0, 8),)),
        "rate_bias": jnp.clip(jax.random.uniform(streams_of[5], (SECTIONS, HW), jnp.float32, -1.0, 1.0) * level_of(streams_of[5], (SECTIONS, HW), ((0, 8),), -0.4, 0.0), -1.0, 1.0),
        "decay_rate": jnp.clip(jnp.exp(math.log(0.03) - 6.89065 * jax.random.uniform(streams_of[6], (SECTIONS, HW), jnp.float32) ** level_of(streams_of[6], (SECTIONS, HW), ((0, 8),), -0.2, 0.2)), 3.0517578125e-05, 0.03),
        "level_table": jnp.clip(jnp.exp(math.log(2.0) - 2.0794415 * jax.random.uniform(streams_of[7], (SECTIONS, BUCKETS, LEVELS, HW), jnp.float32) ** level_of(streams_of[7], (SECTIONS, BUCKETS, LEVELS, HW), ((0, 8),), -0.2, 0.2)), 0.25, 2.0),
        "level_ids": with_ends(jax.random.randint(streams_of[8], (SECTIONS, TOKENS, LEVELS), 0, BUCKETS), jax.random.fold_in(streams_of[8], 1), 0, BUCKETS - 1).astype(jnp.int32),
        "out_gain": jnp.clip(1.0 + 0.1 * jax.random.normal(streams_of[9], (SECTIONS, HW * P_SIZE), jnp.float32), 0.5, 1.5),
        "out_weight": centred(streams_of[10], (SECTIONS, HW * P_SIZE, D), (HW * P_SIZE) ** -0.5, 0.1875, ((0, 8),)),
    }


EPSILON = 1e-05

def bit_table(rows_here, bits_tok):
    position = jnp.arange(rows_here, dtype=jnp.int32)
    flipped = position[:, None] ^ position[None, :]
    bit_level = jnp.zeros((rows_here, rows_here), jnp.int32)
    for bit_pos in range(bits_tok):
        bit_level = bit_level + (flipped >= 1 << bit_pos).astype(jnp.int32)
    return (bit_level, position[:, None] >= position[None, :])

def nearby_block(queries, key_rows, values, running, level_weight):
    bit_level, causal = bit_table(TOK_DEV, TOK_BITS)
    scores = jnp.dot(queries, key_rows.T, preferred_element_type=jnp.float32)
    by_head = running.T
    exponent = jnp.where(causal[None], by_head[:, :, None] - by_head[:, None, :], -jnp.inf)
    weight_heads = jnp.transpose(level_weight, (2, 0, 1))
    weight = jnp.zeros(exponent.shape, jnp.float32)
    for degree in range(TOK_BITS + 1):
        weight = weight + jnp.where(bit_level[None] == degree, weight_heads[:, :, degree:degree + 1], 0.0)
    mixing = (weight * jnp.exp(exponent) * scores[None]).astype(jnp.bfloat16)
    return jnp.einsum('htu,uhp->thp', mixing.astype(jnp.float32), values.astype(jnp.float32), precision=lax.Precision.HIGHEST)

def apply_layer(stream, norm_gain, value_weight, shared_weight, rate_weight, rate_bias, decay_rate, level_table, level_ids, out_gain, out_weight):
    widened = stream.astype(jnp.float32)
    normed = (widened * lax.rsqrt(lax.optimization_barrier(jnp.mean(widened * widened, axis=-1, keepdims=True)) + EPSILON) * norm_gain).astype(jnp.bfloat16)
    values_raw = jnp.dot(normed, value_weight, preferred_element_type=jnp.float32)
    shared_raw = jnp.dot(normed, shared_weight, preferred_element_type=jnp.float32)
    rates_raw = jnp.dot(normed, rate_weight, preferred_element_type=jnp.float32)
    step_size = jax.nn.softplus(rates_raw + rate_bias)
    log_decay = -decay_rate * step_size
    running = jnp.cumsum(log_decay.reshape(N_SEQ, TOK_DEV, HW), axis=1)
    block_decay = running[:, -1, :]
    starts = jnp.cumsum(block_decay, axis=0) - block_decay
    values = (values_raw.reshape(TOKENS, HW, P_SIZE) * step_size[:, :, None]).astype(jnp.bfloat16).reshape(N_SEQ, TOK_DEV, HW, P_SIZE)
    key_rows = shared_raw[:, :N].astype(jnp.bfloat16).reshape(N_SEQ, TOK_DEV, N)
    queries = shared_raw[:, N:].astype(jnp.bfloat16).reshape(N_SEQ, TOK_DEV, N)
    level_weight = level_table[level_ids, jnp.arange(LEVELS, dtype=jnp.int32)[None, :]].reshape(N_SEQ, TOK_DEV, LEVELS, HW)
    decayed = (values.astype(jnp.float32) * jnp.exp(block_decay[:, None, :] - running)[..., None]).astype(jnp.bfloat16)
    states = jnp.einsum('jun,juhp->jhnp', key_rows.astype(jnp.float32), decayed.astype(jnp.float32), precision=lax.Precision.HIGHEST)
    nearby = lax.map(lambda item: nearby_block(*item), (queries, key_rows, values, running, level_weight))
    block_ids = jnp.arange(N_SEQ, dtype=jnp.int32)
    ends = starts + block_decay

    def distant_block(item):
        block_index, query_blk, running_blk, weight_blk, start_blk = item
        found = []
        for degree in range(SEQ_BITS):
            member = (block_ids >> degree + 1 == block_index >> degree + 1) & (block_ids >> degree & 1 == 0) & (block_index >> degree & 1 == 1)
            exponent = jnp.where(member[:, None], start_blk[None, :] - ends, 0.0)
            factor = jnp.where(member[:, None], jnp.exp(exponent), 0.0)
            found.append(jnp.einsum('jh,jhnp->hnp', factor, states, precision=lax.Precision.HIGHEST))
        stacked = jnp.stack(found, axis=1).reshape(HW, SEQ_BITS * N, P_SIZE)
        query_coef = weight_blk[:, TOK_BITS + 1:, :] * jnp.exp(running_blk)[:, None, :]
        scaled = (query_blk.astype(jnp.float32)[:, None, None, :] * jnp.transpose(query_coef, (0, 2, 1))[:, :, :, None]).reshape(TOK_DEV, HW, SEQ_BITS * N)
        return jnp.einsum('thk,hkp->thp', scaled, stacked, precision=lax.Precision.HIGHEST)
    distant = lax.map(distant_block, (block_ids, queries, running, level_weight, starts))
    mixed = (nearby + distant).reshape(TOKENS, HW * P_SIZE)
    normed_mix = (mixed * lax.rsqrt(lax.optimization_barrier(jnp.mean(mixed * mixed, axis=-1, keepdims=True)) + EPSILON) * out_gain).astype(jnp.bfloat16)
    return (widened + jnp.dot(normed_mix, out_weight, preferred_element_type=jnp.float32)).astype(jnp.bfloat16)

def reference(activations, norm_gain, value_weight, shared_weight, rate_weight, rate_bias, decay_rate, level_table, level_ids, out_gain, out_weight):
    params = (norm_gain, value_weight, shared_weight, rate_weight, rate_bias, decay_rate, level_table, level_ids, out_gain, out_weight)
    handed = lax.map(lambda item: apply_layer(item[0], *item[1:]), (activations,) + params)
    arrived = jnp.roll(handed, 1, axis=0)
    return lax.map(lambda item: apply_layer(item[0], *item[1:]), (arrived,) + params)
```

```python
import functools

import jax
import jax.numpy as jnp
from jax import lax
from jax.experimental import pallas as pl
from jax.experimental.pallas import tpu as pltpu
from jax.sharding import PartitionSpec as P

EPSILON = 1e-05
F32 = jnp.float32
BF16 = jnp.bfloat16
HEADS = 8
LANES = 128
BASE = 128
EXTRA = 16


def params(limit_mib=24):
    return pltpu.CompilerParams(vmem_limit_bytes=limit_mib << 20)


def iota(shape, dim):
    return lax.broadcasted_iota(jnp.int32, shape, dim)


def mm(a, b):
    return jnp.dot(a, b, preferred_element_type=F32)


def pieces(v, count):
    out = []
    for _ in range(count):
        top = v.astype(BF16)
        out.append(top)
        v = v - top.astype(F32)
    return out


def spread(first, first_head, width):
    return (
        iota((LANES, width), 0) == iota((LANES, width), 1) // LANES + (first + first_head)
    ).astype(BF16)


def expand(v, sel):
    top, low = pieces(v, 2)
    return mm(top, sel) + mm(low, sel)


def softplus(u):
    return jnp.maximum(u, 0.0) + jnp.log1p(jnp.exp(-jnp.abs(u)))


def weights_kernel(ids_ref, table_ref, out_ref):
    ids = ids_ref[...].astype(F32).astype(BF16)
    levels, buckets = ids.shape[1], 16
    wide = levels * buckets
    rep = (iota((levels, wide), 0) == iota((levels, wide), 1) // buckets).astype(BF16)
    bucket = mm(ids, rep)
    onehot = (bucket == (iota((1, wide), 1) % buckets).astype(F32)).astype(BF16)
    keep = iota((wide, LANES), 0) // buckets == iota((wide, LANES), 1) // HEADS
    tile = (iota((HEADS, LANES), 0) == iota((HEADS, LANES), 1) % HEADS).astype(BF16)
    total = jnp.zeros(out_ref.shape, F32)
    for piece in pieces(table_ref[...], 3):
        block = jnp.where(keep, mm(piece, tile), 0.0).astype(BF16)
        total = total + mm(onehot, block)
    out_ref[...] = total


def level_weights(level_ids, level_table):
    rows, levels = level_ids.shape
    table = jnp.transpose(level_table, (1, 0, 2)).reshape(-1, HEADS)
    return pl.pallas_call(
        weights_kernel,
        out_shape=jax.ShapeDtypeStruct((rows, LANES), F32),
        compiler_params=params(),
        name="weights",
    )(level_ids, table)


def project_kernel(
    x_ref, gain_ref, wv_ref, ws_ref, wr_ref, bias_ref, rate_ref, v_ref, kq_ref, ld_ref, n_s, s_s
):
    j = pl.program_id(0)
    width = wv_ref.shape[1]

    @pl.when(j == 0)
    def _():
        x = x_ref[...].astype(F32)
        mean = jnp.mean(x * x, axis=-1, keepdims=True)
        normed = (x * lax.rsqrt(mean + EPSILON) * gain_ref[...]).astype(BF16)
        n_s[...] = normed
        kq_ref[...] = mm(normed, ws_ref[...]).astype(BF16)
        step = softplus(mm(normed, wr_ref[...]) + bias_ref[...])
        s_s[...] = step
        ld_ref[...] = -rate_ref[...] * step

    sel = spread(0, j * (width // LANES), width)
    v_ref[...] = (mm(n_s[...], wv_ref[...]) * expand(s_s[...], sel)).astype(BF16)


def project(x, gain, wv, ws, wr, bias, rate, width=256):
    rows, depth = x.shape
    heads = wv.shape[1]
    whole = lambda a: pl.BlockSpec(a.shape, lambda j: (0, 0))
    return pl.pallas_call(
        project_kernel,
        grid=(heads // width,),
        in_specs=[
            whole(x),
            whole(gain),
            pl.BlockSpec((depth, width), lambda j: (0, j)),
            whole(ws),
            whole(wr),
            whole(bias),
            whole(rate),
        ],
        out_specs=[
            pl.BlockSpec((rows, width), lambda j: (0, j)),
            pl.BlockSpec((rows, ws.shape[1]), lambda j: (0, 0)),
            pl.BlockSpec((rows, LANES), lambda j: (0, 0)),
        ],
        out_shape=[
            jax.ShapeDtypeStruct((rows, heads), BF16),
            jax.ShapeDtypeStruct((rows, ws.shape[1]), BF16),
            jax.ShapeDtypeStruct((rows, LANES), F32),
        ],
        scratch_shapes=[pltpu.VMEM((rows, depth), BF16), pltpu.VMEM((rows, LANES), F32)],
        compiler_params=params(32),
        cost_estimate=pl.CostEstimate(
            flops=2 * rows * depth * 1408, bytes_accessed=9 << 20, transcendentals=0
        ),
        name="project",
    )(x, gain, wv, ws, wr, bias, rate)


def contract_rows(a, b):
    return lax.dot_general(a, b, (((0,), (0,)), ((), ())), preferred_element_type=F32)


def state_kernel(groups, ld_ref, kq_ref, v_ref, run_ref, runt_ref, *pay_refs):
    rows = ld_ref.shape[0]
    lower = (iota((rows, rows), 0) >= iota((rows, rows), 1)).astype(BF16)
    run = jnp.zeros(ld_ref.shape, F32)
    for piece in pieces(ld_ref[...], 3):
        run = run + mm(lower, piece)
    run_ref[...] = run
    runt_ref[...] = run.T
    last = run[rows - 1 : rows, :]
    fade = jnp.exp(last - run)
    keys = kq_ref[:, :LANES]
    width = v_ref.shape[1] // groups
    for g in range(groups):
        sel = spread(0, g * (width // LANES), width)
        cut = slice(g * width, (g + 1) * width)
        decayed = (v_ref[:, cut].astype(F32) * expand(fade, sel)).astype(BF16)
        pay_refs[g][:LANES, :] = contract_rows(keys, decayed).astype(BF16)
        top, low = pieces(jnp.broadcast_to(last, (EXTRA, LANES)), 2)
        row = iota((EXTRA, width), 0)
        both = jnp.where(row == 0, mm(top, sel), jnp.where(row == 1, mm(low, sel), 0.0))
        pay_refs[g][LANES:, :] = both.astype(BF16)


def block_state(ld, kq, values, groups):
    rows = ld.shape[0]
    width = values.shape[1] // groups
    return pl.pallas_call(
        functools.partial(state_kernel, groups),
        out_shape=[
            jax.ShapeDtypeStruct((rows, LANES), F32),
            jax.ShapeDtypeStruct((LANES, rows), F32),
        ]
        + [jax.ShapeDtypeStruct((LANES + EXTRA, width), BF16)] * groups,
        compiler_params=params(),
        cost_estimate=pl.CostEstimate(
            flops=2 * rows * LANES * values.shape[1] * 4, bytes_accessed=2 << 20, transcendentals=0
        ),
        name="state",
    )(ld, kq, values)


def nearby_kernel(first_head, kq_ref, v_ref, run_ref, runt_ref, lw_ref, out_ref):
    rows, width = out_ref.shape
    heads = width // LANES
    run = run_ref[...]
    weights = lw_ref[...]
    blocks = rows // BASE
    depth = BASE.bit_length() - 1
    flipped = iota((BASE, BASE), 0) ^ iota((BASE, BASE), 1)
    causal = iota((BASE, BASE), 0) >= iota((BASE, BASE), 1)
    for block in range(blocks):
        here = slice(block * BASE, (block + 1) * BASE)
        keys, queries = kq_ref[here, :LANES], kq_ref[here, LANES:]
        scores = lax.dot_general(
            queries, keys, (((1,), (1,)), ((), ())), preferred_element_type=F32
        )
        for head in range(heads):
            true_head = first_head + head
            weight = jnp.broadcast_to(weights[here, true_head : true_head + 1], (BASE, BASE))
            for bit in range(depth):
                column = (bit + 1) * HEADS + true_head
                weight = jnp.where(flipped >= 1 << bit, weights[here, column : column + 1], weight)
            gap = run[here, true_head : true_head + 1] - runt_ref[true_head : true_head + 1, here]
            fade = jnp.exp(jnp.where(causal, gap, -jnp.inf))
            mixing = (weight * fade * scores).astype(BF16)
            lanes = slice(head * LANES, (head + 1) * LANES)
            out_ref[here, lanes] = mm(mixing, v_ref[here, lanes])
    span = BASE
    level = depth + 1
    while span < rows:
        sel_now = spread(0, first_head, width)
        sel_level = spread(level * HEADS, first_head, width)
        for start in range(0, rows, 2 * span):
            low = slice(start, start + span)
            high = slice(start + span, start + 2 * span)
            turn = run[start + span - 1 : start + span, :]
            faded = (v_ref[low, :].astype(F32) * expand(jnp.exp(turn - run[low, :]), sel_now)).astype(
                BF16
            )
            state = contract_rows(kq_ref[low, :LANES], faded).astype(BF16)
            coef = weights[high, :] * jnp.exp(run[high, :] - turn)
            out_ref[high, :] = out_ref[high, :] + expand(coef, sel_level) * mm(
                kq_ref[high, LANES:], state
            )
        span *= 2
        level += 1


def nearby(kq, values, run, runt, weights, part, parts):
    rows = kq.shape[0]
    width = values.shape[1] // parts
    whole = lambda a: pl.BlockSpec(a.shape, lambda i: (0, 0))
    return pl.pallas_call(
        functools.partial(nearby_kernel, part * (width // LANES)),
        grid=(1,),
        in_specs=[
            whole(kq),
            pl.BlockSpec((rows, width), lambda i: (0, part)),
            whole(run),
            whole(runt),
            whole(weights),
        ],
        out_specs=pl.BlockSpec((rows, width), lambda i: (0, 0)),
        out_shape=jax.ShapeDtypeStruct((rows, width), F32),
        compiler_params=params(),
        cost_estimate=pl.CostEstimate(
            flops=900_000_000 // parts, bytes_accessed=3 << 20, transcendentals=0
        ),
        name="nearby",
    )(kq, values, run, runt, weights)


def decay_of(pay_ref):
    tail = pay_ref[LANES:, :].astype(F32)
    return tail[0:1, :] + tail[1:2, :]


def merge_kernel(bit, index_ref, own_ref, other_ref, out_ref):
    upper = (index_ref[0] >> bit & 1) == 1
    own, other = decay_of(own_ref), decay_of(other_ref)
    keep = jnp.exp(jnp.where(upper, 0.0, other))
    take = jnp.exp(jnp.where(upper, own, 0.0))
    out_ref[:LANES, :] = (
        own_ref[:LANES, :].astype(F32) * keep + other_ref[:LANES, :].astype(F32) * take
    ).astype(BF16)
    top, low = pieces(own + other, 2)
    row = iota((EXTRA, own.shape[1]), 0)
    both = jnp.where(row == 0, top.astype(F32), jnp.where(row == 1, low.astype(F32), 0.0))
    out_ref[LANES:, :] = both.astype(BF16)


SMEM_SPEC = pl.BlockSpec(memory_space=pltpu.SMEM)
FULL = pl.BlockSpec(memory_space=pltpu.VMEM)


def merge(bit, index, own, other):
    return pl.pallas_call(
        functools.partial(merge_kernel, bit),
        in_specs=[SMEM_SPEC, FULL, FULL],
        out_specs=FULL,
        out_shape=jax.ShapeDtypeStruct(own.shape, BF16),
        compiler_params=params(8),
        cost_estimate=pl.CostEstimate(flops=1 << 20, bytes_accessed=1 << 20, transcendentals=0),
        name="merge",
    )(index, own, other)


def partners(bit, last, seq):
    if last:
        half = seq // 2
        group = seq // 4
        route = []
        for i in range(half):
            row, col = divmod(i, group)
            route.append((i, half + (1 - row) * group + col))
        return route
    return [(i, i ^ 1 << bit) for i in range(seq)]


def distant_levels_kernel(bits, tok_bits, head0, index_ref, kq_ref, run_ref, lw_ref, near_ref, *refs):
    out_ref = refs[bits]
    before_ref = refs[bits + 1]
    width = out_ref.shape[1]
    queries = kq_ref[:, LANES:]
    coef = lw_ref[...] * jnp.exp(run_ref[...])
    before = jnp.zeros((1, width), F32)
    total = near_ref[...]
    for bit in range(bits):
        upper = (index_ref[0] >> bit & 1) == 1
        factor = jnp.where(upper, jnp.exp(before), 0.0)
        far = (refs[bit][:LANES, :].astype(F32) * factor).astype(BF16)
        sel = spread((tok_bits + 1 + bit) * HEADS, head0, width)
        total = total + expand(coef, sel) * mm(queries, far)
        before = before + jnp.where(upper, decay_of(refs[bit]), 0.0)
    out_ref[...] = total
    before_ref[...] = jnp.broadcast_to(before, before_ref.shape)


def distant_levels(index, kq, run, weights, near, arrived, tok_bits, head0):
    rows, width = near.shape
    bits = len(arrived)
    return pl.pallas_call(
        functools.partial(distant_levels_kernel, bits, tok_bits, head0),
        in_specs=[SMEM_SPEC] + [FULL] * (4 + bits),
        out_specs=[FULL, FULL],
        out_shape=[
            jax.ShapeDtypeStruct((rows, width), F32),
            jax.ShapeDtypeStruct((8, width), F32),
        ],
        compiler_params=params(),
        cost_estimate=pl.CostEstimate(
            flops=2 * rows * LANES * width * bits * 4, bytes_accessed=6 << 20, transcendentals=0
        ),
        name="distant",
    )(index, kq, run, weights, near, *arrived)


def finish_kernel(groups, column, kq_ref, run_ref, lw_ref, gain_ref, x_ref, w_ref, *refs):
    near_refs, before_refs, far_refs = (
        refs[:groups],
        refs[groups : 2 * groups],
        refs[2 * groups : 3 * groups],
    )
    out_ref = refs[3 * groups]
    queries = kq_ref[:, LANES:]
    coef = lw_ref[...] * jnp.exp(run_ref[...])
    mixed = []
    squares = 0.0
    width = near_refs[0].shape[1]
    for g in range(groups):
        far = (far_refs[g][:LANES, :].astype(F32) * jnp.exp(before_refs[g][0:1, :])).astype(BF16)
        sel = spread(column, g * (width // LANES), width)
        part = near_refs[g][...] + expand(coef, sel) * mm(queries, far)
        squares = squares + jnp.sum(part * part, axis=-1, keepdims=True)
        mixed.append(part)
    scale = lax.rsqrt(squares / (groups * width) + EPSILON)
    total = x_ref[...].astype(F32)
    for g in range(groups):
        cut = slice(g * width, (g + 1) * width)
        normed = (mixed[g] * scale * gain_ref[:, cut]).astype(BF16)
        total = total + mm(normed, w_ref[cut, :])
    out_ref[...] = total.astype(BF16)


def finish(chunk, chunks, kq, run, weights, gain, x, w, near, before, far, column):
    rows = kq.shape[0] // chunks
    groups = len(near)
    part = lambda a: pl.BlockSpec((rows, a.shape[1]), lambda i: (chunk, 0))
    whole = lambda a: pl.BlockSpec(a.shape, lambda i: (0, 0))
    xs = part(x) if x.shape[0] != rows else whole(x)
    return pl.pallas_call(
        functools.partial(finish_kernel, groups, column),
        grid=(1,),
        in_specs=[part(kq), part(run), part(weights), whole(gain), xs, whole(w)]
        + [part(a) for a in near]
        + [whole(a) for a in before]
        + [whole(a) for a in far],
        out_specs=pl.BlockSpec((rows, x.shape[1]), lambda i: (0, 0)),
        out_shape=jax.ShapeDtypeStruct((rows, x.shape[1]), BF16),
        compiler_params=params(32),
        cost_estimate=pl.CostEstimate(
            flops=2 * rows * w.shape[0] * w.shape[1], bytes_accessed=8 << 20, transcendentals=0
        ),
        name="finish",
    )(kq, run, weights, gain, x, w, *near, *before, *far)


GROUPS = 2
CHUNKS_OUT = 2


def apply_layer(xs, p, index, weights):
    chunks = len(xs)
    projected = [
        project(x, p["gain"], p["wv"], p["ws"], p["wr"], p["bias"], p["rate"]) for x in xs
    ]
    values, kq, ld = [
        parts[0] if chunks == 1 else jnp.concatenate(parts, axis=0) for parts in zip(*projected)
    ]
    rows = kq.shape[0]
    tok_bits = rows.bit_length() - 1
    run, runt, *own = block_state(ld, kq, values, GROUPS)
    seq = lax.axis_size("seq")
    bits = seq.bit_length() - 1
    arrived = [[] for _ in range(GROUPS)]
    for bit in range(bits):
        last = bit == bits - 1
        for g in range(GROUPS):
            other = lax.ppermute(own[g], "seq", partners(bit, last, seq))
            arrived[g].append(other)
            if not last:
                own[g] = merge(bit, index, own[g], other)
    near, before = [], []
    for g in range(GROUPS):
        near_g = nearby(kq, values, run, runt, weights, g, GROUPS)
        head0 = g * (HEADS // GROUPS)
        acc, pre = distant_levels(
            index, kq, run, weights, near_g, arrived[g][:-1], tok_bits, head0
        )
        near.append(acc)
        before.append(pre)
    far = [a[-1] for a in arrived]
    column = (tok_bits + bits) * HEADS
    outs = []
    out_chunks = CHUNKS_OUT
    for c in range(out_chunks):
        x = xs[0] if len(xs) == 1 else xs[c]
        outs.append(
            finish(c, out_chunks, kq, run, weights, p["out_gain"], x, p["wo"], near, before, far, column)
        )
    return outs


def body(
    activations,
    norm_gain,
    value_weight,
    shared_weight,
    rate_weight,
    rate_bias,
    decay_rate,
    level_table,
    level_ids,
    out_gain,
    out_weight,
):
    tiled = LANES // HEADS
    p = {
        "gain": norm_gain,
        "wv": value_weight[0],
        "ws": shared_weight[0],
        "wr": jnp.tile(rate_weight[0], (1, tiled)),
        "bias": jnp.tile(rate_bias, (1, tiled)),
        "rate": jnp.tile(decay_rate, (1, tiled)),
        "out_gain": out_gain,
        "wo": out_weight[0],
    }
    index = lax.axis_index("seq").astype(jnp.int32).reshape(1)
    weights = level_weights(level_ids[0], level_table[0])
    handed = apply_layer([activations[0]], p, index, weights)
    count = lax.axis_size("section")
    route = [(i, (i + 1) % count) for i in range(count)]
    arrived = [lax.ppermute(h, "section", route) for h in handed]
    result = apply_layer(arrived, p, index, weights)
    return jnp.concatenate(result, axis=0)[None]


def solution(mesh):
    placed = (
        P("section", "seq", None),
        P("section", None),
        P("section", None, None),
        P("section", None, None),
        P("section", None, None),
        P("section", None),
        P("section", None),
        P("section", None, None, None),
        P("section", "seq", None),
        P("section", None),
        P("section", None, None),
    )
    return jax.shard_map(
        body, mesh=mesh, in_specs=placed, out_specs=P("section", "seq", None), check_vma=False
    )
```

```python
import functools

import jax
import jax.numpy as jnp
from jax import lax
from jax.experimental import pallas as pl
from jax.experimental.pallas import tpu as pltpu
from jax.sharding import PartitionSpec as P

EPSILON = 1e-05
F32 = jnp.float32
BF16 = jnp.bfloat16
HEADS = 8
LANES = 128
BASE = 128
EXTRA = 16


def params(limit_mib=24):
    return pltpu.CompilerParams(vmem_limit_bytes=limit_mib << 20)


def iota(shape, dim):
    return lax.broadcasted_iota(jnp.int32, shape, dim)


def scalar(value):
    return jnp.full((1,), value, jnp.int32)


def mm(a, b):
    return jnp.dot(a, b, preferred_element_type=F32)


def pieces(v, count):
    out = []
    for _ in range(count):
        top = v.astype(BF16)
        out.append(top)
        v = v - top.astype(F32)
    return out


def spread(first, first_head, width):
    return (
        iota((LANES, width), 0) == iota((LANES, width), 1) // LANES + (first + first_head)
    ).astype(BF16)


def expand(v, sel):
    top, low = pieces(v, 2)
    return mm(top, sel) + mm(low, sel)


def softplus(u):
    return jnp.maximum(u, 0.0) + jnp.log1p(jnp.exp(-jnp.abs(u)))


def weights_kernel(ids_ref, table_ref, out_ref):
    ids = ids_ref[...].astype(F32).astype(BF16)
    levels, buckets = ids.shape[1], 16
    wide = levels * buckets
    rep = (iota((levels, wide), 0) == iota((levels, wide), 1) // buckets).astype(BF16)
    bucket = mm(ids, rep)
    onehot = (bucket == (iota((1, wide), 1) % buckets).astype(F32)).astype(BF16)
    keep = iota((wide, LANES), 0) // buckets == iota((wide, LANES), 1) // HEADS
    tile = (iota((HEADS, LANES), 0) == iota((HEADS, LANES), 1) % HEADS).astype(BF16)
    total = jnp.zeros(out_ref.shape, F32)
    for piece in pieces(table_ref[...], 3):
        block = jnp.where(keep, mm(piece, tile), 0.0).astype(BF16)
        total = total + mm(onehot, block)
    out_ref[...] = total


def level_weights(level_ids, level_table):
    rows, levels = level_ids.shape
    table = jnp.transpose(level_table, (1, 0, 2)).reshape(-1, HEADS)
    return pl.pallas_call(
        weights_kernel,
        out_shape=jax.ShapeDtypeStruct((rows, LANES), F32),
        compiler_params=params(),
        name="weights",
    )(level_ids, table)


def project_kernel(first, rows, *refs):
    start = 0
    if first:
        x_hbm, gain_ref, wv_hbm, ws_hbm, wrt_ref, bias_ref, rate_ref = refs[:7]
        v_ref, kq_ref, wrt_out, bias_out, rate_out, run_ref = refs[7:13]
        pay_refs = refs[13 : 13 + GROUPS]
        ld_ref, x_s, wv_s, ws_s, n_s, s_s, x_sem, wv_sem, ws_sem = refs[13 + GROUPS :]
        quarter = rows // 4
        x_copies = [
            pltpu.make_async_copy(
                x_hbm.at[pl.ds(k * quarter, quarter), :],
                x_s.at[pl.ds(k * quarter, quarter), :],
                x_sem.at[k],
            )
            for k in range(4)
        ]
        ws_copy = pltpu.make_async_copy(ws_hbm, ws_s, ws_sem)
        wv_copies = [
            pltpu.make_async_copy(
                wv_hbm.at[:, pl.ds(k * CHUNK, CHUNK)], wv_s.at[k], wv_sem.at[k]
            )
            for k in range(wv_s.shape[0])
        ]
        for copy in x_copies + [ws_copy] + wv_copies:
            copy.start()
        tile = (iota((HEADS, LANES), 0) == iota((HEADS, LANES), 1) % HEADS).astype(BF16)
        wrt_out[...] = contract_rows(tile, wrt_ref[...]).astype(BF16)
        for small_ref, wide_ref in ((bias_ref, bias_out), (rate_ref, rate_out)):
            wide = 0.0
            for piece in pieces(jnp.broadcast_to(small_ref[...], (HEADS, HEADS)), 3):
                wide = wide + mm(piece, tile)
            wide_ref[...] = wide
        wrt_ref, bias_ref, rate_ref, ws_ref = wrt_out, bias_out, rate_out, ws_s
        for copy in x_copies:
            copy.wait()
        normalize(x_s, gain_ref, n_s)
        ws_copy.wait()
        columns = wv_s.shape[0]
    else:
        start_ref, x_ref, gain_ref, wv_ref, ws_ref, wrt_ref, bias_ref, rate_ref = refs[:8]
        v_ref, kq_ref, ld_ref, x_all = refs[-6:-2]
        n_s, s_s = refs[-2:]
        start = pl.multiple_of(start_ref[0], BASE)
        x_all[pl.ds(start, rows), :] = x_ref[...]
        normalize(x_ref, gain_ref, n_s)
        columns = wv_ref.shape[1] // CHUNK
    block = min(rows, 2 * BASE)

    def shared(i, carry):
        here = pl.ds(pl.multiple_of(i * block, block), block)
        out = pl.ds(pl.multiple_of(start + i * block, BASE), block)
        normed = n_s[here, :]
        kq_ref[out, :] = mm(normed, ws_ref[...]).astype(BF16)
        rates = lax.dot_general(
            normed, wrt_ref[...], (((1,), (1,)), ((), ())), preferred_element_type=F32
        )
        step = softplus(rates + bias_ref[0:1, :])
        s_s[here, :] = step
        ld_ref[out, :] = -rate_ref[0:1, :] * step
        return carry

    lax.fori_loop(0, rows // block, shared, 0)
    if first:
        for copy in wv_copies:
            copy.wait()

    def column(k, carry):
        j, i = k // (rows // block), k % (rows // block)
        here = pl.ds(pl.multiple_of(i * block, block), block)
        out = pl.ds(pl.multiple_of(start + i * block, BASE), block)
        cut = pl.ds(pl.multiple_of(j * CHUNK, CHUNK), CHUNK)
        weight = wv_s[j] if first else wv_ref[:, cut]
        sel = spread(0, j * (CHUNK // LANES), CHUNK)
        v_ref[out, cut] = (mm(n_s[here, :], weight) * expand(s_s[here, :], sel)).astype(BF16)
        return carry

    lax.fori_loop(0, columns * (rows // block), column, 0)
    if first:
        state_kernel(GROUPS, ld_ref, kq_ref, v_ref, run_ref, *pay_refs)


def normalize(x_ref, gain_ref, out_ref):
    step = 32

    def block(i, carry):
        here = pl.ds(pl.multiple_of(i * step, step), step)
        x = x_ref[here, :].astype(F32)
        mean = jnp.mean(x * x, axis=-1, keepdims=True)
        out_ref[here, :] = (x * lax.rsqrt(mean + EPSILON) * gain_ref[...]).astype(BF16)
        return carry

    lax.fori_loop(0, x_ref.shape[0] // step, block, 0)


CHUNK = 256
HBM_SPEC = pl.BlockSpec(memory_space=pltpu.HBM)
SMEM_SPEC = pl.BlockSpec(memory_space=pltpu.SMEM)
FULL = pl.BlockSpec(memory_space=pltpu.VMEM)
KEPT = pl.BlockSpec(memory_space=pl.ANY)


def project_first(x, p):
    rows, depth = x.shape
    heads = p["wv"].shape[1]
    shared = p["ws"].shape[1]
    return pl.pallas_call(
        functools.partial(project_kernel, True, rows),
        in_specs=[HBM_SPEC, FULL, HBM_SPEC, HBM_SPEC, FULL, FULL, FULL],
        out_specs=[FULL] * (6 + GROUPS),
        out_shape=[
            jax.ShapeDtypeStruct((rows, heads), BF16),
            jax.ShapeDtypeStruct((rows, shared), BF16),
            jax.ShapeDtypeStruct((LANES, depth), BF16),
            jax.ShapeDtypeStruct((HEADS, LANES), F32),
            jax.ShapeDtypeStruct((HEADS, LANES), F32),
            jax.ShapeDtypeStruct((rows, LANES), F32),
        ]
        + [jax.ShapeDtypeStruct((LANES + EXTRA, heads // GROUPS), BF16)] * GROUPS,
        scratch_shapes=[
            pltpu.VMEM((rows, LANES), F32),
            pltpu.VMEM((rows, depth), BF16),
            pltpu.VMEM((heads // CHUNK, depth, CHUNK), BF16),
            pltpu.VMEM((depth, shared), BF16),
            pltpu.VMEM((rows, depth), BF16),
            pltpu.VMEM((rows, LANES), F32),
            pltpu.SemaphoreType.DMA((4,)),
            pltpu.SemaphoreType.DMA((heads // CHUNK,)),
            pltpu.SemaphoreType.DMA,
        ],
        compiler_params=params(56),
        cost_estimate=pl.CostEstimate(
            flops=2 * rows * depth * 1408, bytes_accessed=9 << 20, transcendentals=0
        ),
        name="project",
    )(x, p["gain"], p["wv"], p["ws"], p["wr"], p["bias"], p["rate"])


def project_next(chunk, rows, x, p, before):
    part, depth = x.shape
    heads = p["wv"].shape[1]
    shared = p["ws"].shape[1]
    inputs = [scalar(chunk * part), x, p["gain"], p["wv"], p["ws"], p["wr128"], p["bias128"], p["rate128"]]
    return pl.pallas_call(
        functools.partial(project_kernel, False, part),
        in_specs=[SMEM_SPEC] + [FULL] * (len(inputs) - 1 + len(before)),
        out_specs=[FULL] * 4,
        out_shape=[
            jax.ShapeDtypeStruct((rows, heads), BF16),
            jax.ShapeDtypeStruct((rows, shared), BF16),
            jax.ShapeDtypeStruct((rows, LANES), F32),
            jax.ShapeDtypeStruct((rows, depth), BF16),
        ],
        input_output_aliases={len(inputs) + k: k for k in range(len(before))},
        scratch_shapes=[pltpu.VMEM((part, depth), BF16), pltpu.VMEM((part, LANES), F32)],
        compiler_params=params(16),
        cost_estimate=pl.CostEstimate(
            flops=2 * part * depth * 1408, bytes_accessed=7 << 20, transcendentals=0
        ),
        name="project",
    )(*inputs, *before)


def contract_rows(a, b):
    return lax.dot_general(a, b, (((0,), (0,)), ((), ())), preferred_element_type=F32)


def state_kernel(groups, ld_ref, kq_ref, v_ref, run_ref, *pay_refs):
    rows = ld_ref.shape[0]
    lower = (iota((BASE, BASE), 0) >= iota((BASE, BASE), 1)).astype(BF16)
    last = jnp.zeros((1, LANES), F32)
    runs = []
    for block in range(rows // BASE):
        here = slice(block * BASE, (block + 1) * BASE)
        run = jnp.broadcast_to(last, (BASE, LANES))
        for piece in pieces(ld_ref[here, :], 3):
            run = run + mm(lower, piece)
        run_ref[here, :] = run
        last = run[BASE - 1 :, :]
    fade = jnp.exp(last - run_ref[...])
    keys = kq_ref[:, :LANES]
    width = v_ref.shape[1] // groups
    for g in range(groups):
        sel = spread(0, g * (width // LANES), width)
        cut = slice(g * width, (g + 1) * width)
        decayed = (v_ref[:, cut].astype(F32) * expand(fade, sel)).astype(BF16)
        pay_refs[g][:LANES, :] = contract_rows(keys, decayed).astype(BF16)
        top, low = pieces(jnp.broadcast_to(last, (EXTRA, LANES)), 2)
        row = iota((EXTRA, width), 0)
        both = jnp.where(row == 0, mm(top, sel), jnp.where(row == 1, mm(low, sel), 0.0))
        pay_refs[g][LANES:, :] = both.astype(BF16)


def block_state(ld, kq, values, groups):
    rows = ld.shape[0]
    width = values.shape[1] // groups
    return pl.pallas_call(
        functools.partial(state_kernel, groups),
        in_specs=[FULL] * 3,
        out_specs=[FULL] * (1 + groups),
        out_shape=[jax.ShapeDtypeStruct((rows, LANES), F32)]
        + [jax.ShapeDtypeStruct((LANES + EXTRA, width), BF16)] * groups,
        compiler_params=params(16),
        cost_estimate=pl.CostEstimate(
            flops=2 * rows * LANES * values.shape[1] * 4, bytes_accessed=2 << 20, transcendentals=0
        ),
        name="state",
    )(ld, kq, values)


def nearby_kernel(head_ref, kq_ref, v_ref, run_ref, lw_ref, *refs):
    out_ref, lws, runs, turned = refs[-4:]
    rows, width = out_ref.shape
    heads = width // LANES
    depth = BASE.bit_length() - 1
    first_head = head_ref[0]
    source, target = iota((LANES, LANES), 0), iota((LANES, LANES), 1)
    pick = (source == target % 16 * HEADS + first_head + target // 16).astype(BF16)
    same = (source == first_head + target // 16).astype(BF16)
    lws[...] = sum(mm(piece, pick) for piece in pieces(lw_ref[...], 2))
    mine = sum(mm(piece, same) for piece in pieces(run_ref[...], 3))
    runs[...] = mine
    turned[...] = mine.T

    def diagonal(block, carry):
        here = pl.ds(pl.multiple_of(block * BASE, BASE), BASE)
        flipped = iota((BASE, BASE), 0) ^ iota((BASE, BASE), 1)
        causal = iota((BASE, BASE), 0) >= iota((BASE, BASE), 1)
        scores = lax.dot_general(
            kq_ref[here, LANES:], kq_ref[here, :LANES], (((1,), (1,)), ((), ())),
            preferred_element_type=F32,
        )
        weights, run = lws[here, :], runs[here, :]
        for head in range(heads):
            column = head * 16
            weight = jnp.broadcast_to(weights[:, column : column + 1], (BASE, BASE))
            for bit in range(depth):
                level = column + bit + 1
                weight = jnp.where(flipped >= 1 << bit, weights[:, level : level + 1], weight)
            gap = run[:, column : column + 1] - turned[column : column + 1, here]
            fade = jnp.exp(jnp.where(causal, gap, -jnp.inf))
            mixing = (weight * fade * scores).astype(BF16)
            lanes = pl.ds(pl.multiple_of((first_head + head) * LANES, LANES), LANES)
            out_ref[here, head * LANES : (head + 1) * LANES] = mm(mixing, v_ref[here, lanes])
        return carry

    lax.fori_loop(0, rows // BASE, diagonal, 0)
    columns = pl.ds(pl.multiple_of(first_head * LANES, LANES), width)
    span = BASE
    level = depth + 1
    while span < rows:
        sel_now = spread(0, first_head, width)
        sel_level = spread(level * HEADS, first_head, width)
        for start in range(0, rows, 2 * span):
            low = slice(start, start + span)
            high = slice(start + span, start + 2 * span)
            turn = run_ref[start + span - 1 : start + span, :]
            fade = expand(jnp.exp(turn - run_ref[low, :]), sel_now)
            faded = (v_ref[low, columns].astype(F32) * fade).astype(BF16)
            state = contract_rows(kq_ref[low, :LANES], faded).astype(BF16)
            coef = lw_ref[high, :] * jnp.exp(run_ref[high, :] - turn)
            out_ref[high, :] = out_ref[high, :] + expand(coef, sel_level) * mm(
                kq_ref[high, LANES:], state
            )
        span *= 2
        level += 1


def nearby(kq, values, run, weights, part, parts, after):
    rows = kq.shape[0]
    width = values.shape[1] // parts
    return pl.pallas_call(
        nearby_kernel,
        in_specs=[SMEM_SPEC] + [FULL] * 4 + [KEPT] * len(after),
        out_specs=FULL,
        out_shape=jax.ShapeDtypeStruct((rows, width), F32),
        scratch_shapes=[pltpu.VMEM((rows, LANES), F32)] * 2 + [pltpu.VMEM((LANES, rows), F32)],
        compiler_params=params(12),
        cost_estimate=pl.CostEstimate(
            flops=4_000_000_000 // parts, bytes_accessed=3 << 20, transcendentals=0
        ),
        name="nearby",
    )(scalar(part * (width // LANES)), kq, values, run, weights, *after)


def decay_of(pay_ref):
    tail = pay_ref[LANES:, :].astype(F32)
    return tail[0:1, :] + tail[1:2, :]


def merge_kernel(bit, index_ref, own_ref, other_ref, *refs):
    out_ref = refs[-1]
    upper = (index_ref[0] >> bit & 1) == 1
    own, other = decay_of(own_ref), decay_of(other_ref)
    keep = jnp.exp(jnp.where(upper, 0.0, other))
    take = jnp.exp(jnp.where(upper, own, 0.0))
    out_ref[:LANES, :] = (
        own_ref[:LANES, :].astype(F32) * keep + other_ref[:LANES, :].astype(F32) * take
    ).astype(BF16)
    top, low = pieces(own + other, 2)
    row = iota((EXTRA, own.shape[1]), 0)
    both = jnp.where(row == 0, top.astype(F32), jnp.where(row == 1, low.astype(F32), 0.0))
    out_ref[LANES:, :] = both.astype(BF16)


def merge(bit, index, own, other, after):
    return pl.pallas_call(
        functools.partial(merge_kernel, bit),
        in_specs=[SMEM_SPEC, FULL, FULL] + [KEPT] * len(after),
        out_specs=FULL,
        out_shape=jax.ShapeDtypeStruct(own.shape, BF16),
        compiler_params=params(8),
        cost_estimate=pl.CostEstimate(flops=1 << 20, bytes_accessed=1 << 20, transcendentals=0),
        name="merge",
    )(index, own, other, *after)


def partners(bit, last, seq, row):
    if last:
        half = seq // 2
        route = []
        for i in range(half):
            line, place = divmod(i, row)
            route.append((i, seq - row * (line + 1) + place))
        return route
    if 2 << bit == row:
        return [(i, i ^ (row - 1)) for i in range(seq)]
    return [(i, i ^ 1 << bit) for i in range(seq)]


def distant_kernel(bits, tok_bits, near_count, has_before, *refs):
    index_ref, head_ref, kq_ref, run_ref, lw_ref = refs[:5]
    near_refs = refs[5 : 5 + near_count]
    rest = refs[5 + near_count :]
    out_ref, before_out = refs[-2:]
    width = out_ref.shape[1]
    queries = kq_ref[:, LANES:]
    coef = lw_ref[...] * jnp.exp(run_ref[...])
    before = rest[len(bits)][0:1, :] if has_before else jnp.zeros((1, width), F32)
    offset = 0
    for near_ref in near_refs:
        part = slice(offset, offset + near_ref.shape[1])
        out_ref[:, part] = near_ref[...]
        offset += near_ref.shape[1]
    total = out_ref[...]
    for k, bit in enumerate(bits):
        upper = (index_ref[0] >> bit & 1) == 1
        factor = jnp.where(upper, jnp.exp(before), 0.0)
        far = (rest[k][:LANES, :].astype(F32) * factor).astype(BF16)
        sel = spread((tok_bits + 1 + bit) * HEADS, head_ref[0], width)
        total = total + expand(coef, sel) * mm(queries, far)
        before = before + jnp.where(upper, decay_of(rest[k]), 0.0)
    out_ref[...] = total
    before_out[...] = jnp.broadcast_to(before, before_out.shape)


def distant(bits, index, kq, run, weights, near, arrived, before, tok_bits, head0):
    rows = kq.shape[0]
    width = arrived[0].shape[1]
    extra = [] if before is None else [before]
    return pl.pallas_call(
        functools.partial(distant_kernel, bits, tok_bits, len(near), bool(extra)),
        in_specs=[SMEM_SPEC] * 2 + [FULL] * (3 + len(near) + len(arrived) + len(extra)),
        out_specs=[FULL, FULL],
        out_shape=[
            jax.ShapeDtypeStruct((rows, width), F32),
            jax.ShapeDtypeStruct((8, width), F32),
        ],
        compiler_params=params(16),
        cost_estimate=pl.CostEstimate(
            flops=8 * rows * LANES * width * len(bits) * 4, bytes_accessed=3 << 20, transcendentals=0
        ),
        name="distant",
    )(index, scalar(head0), kq, run, weights, *near, *arrived, *extra)


def finish_kernel(groups, column, start_ref, kq_ref, run_ref, lw_ref, gain_ref, x_ref, w_ref, *refs):
    near_refs, before_refs, far_refs = (
        refs[:groups],
        refs[groups : 2 * groups],
        refs[2 * groups : 3 * groups],
    )
    out_ref, n_s = refs[3 * groups :]
    rows = out_ref.shape[0]
    first = start_ref[0] + pl.program_id(0) * rows
    here = pl.ds(pl.multiple_of(first, BASE), rows)
    queries = kq_ref[here, LANES:]
    coef = lw_ref[here, :] * jnp.exp(run_ref[here, :])
    mixed = []
    squares = 0.0
    width = near_refs[0].shape[1]
    for g in range(groups):
        far = (far_refs[g][:LANES, :].astype(F32) * jnp.exp(before_refs[g][0:1, :])).astype(BF16)
        sel = spread(column, g * (width // LANES), width)
        part = near_refs[g][here, :] + expand(coef, sel) * mm(queries, far)
        squares = squares + jnp.sum(part * part, axis=-1, keepdims=True)
        mixed.append(part)
    scale = lax.rsqrt(squares / (groups * width) + EPSILON)
    for g in range(groups):
        cut = slice(g * width, (g + 1) * width)
        n_s[:, cut] = (mixed[g] * scale * gain_ref[:, cut]).astype(BF16)

    def columns(j, carry):
        cut = pl.ds(pl.multiple_of(j * WIDE, WIDE), WIDE)
        total = x_ref[here, cut].astype(F32) + mm(n_s[...], w_ref[:, cut])
        out_ref[:, cut] = total.astype(BF16)
        return carry

    lax.fori_loop(0, out_ref.shape[1] // WIDE, columns, 0)


WIDE = 512


def finish(start, rows, steps, kq, run, weights, gain, x, w, near, before, far, column):
    groups = len(near)
    out_spec = (
        FULL if steps == 1 else pl.BlockSpec((rows, x.shape[1]), lambda i: (i, 0))
    )
    return pl.pallas_call(
        functools.partial(finish_kernel, groups, column),
        grid=(steps,),
        in_specs=[SMEM_SPEC] + [FULL] * (6 + 3 * groups),
        out_specs=out_spec,
        out_shape=jax.ShapeDtypeStruct((rows * steps, x.shape[1]), BF16),
        scratch_shapes=[pltpu.VMEM((rows, w.shape[0]), BF16)],
        compiler_params=params(16),
        cost_estimate=pl.CostEstimate(
            flops=2 * rows * w.shape[0] * w.shape[1], bytes_accessed=8 << 20, transcendentals=0
        ),
        name="finish",
    )(scalar(start), kq, run, weights, gain, x, w, *near, *before, *far)


GROUPS = 2
PIECES = 4

PARTS = 4


def held(value, *after):
    return lax.optimization_barrier((value,) + after)[0]


def mix(values, kq, run, a, b, index, weights):
    rows = kq.shape[0]
    tok_bits = rows.bit_length() - 1
    seq = lax.axis_size("seq")
    bits = seq.bit_length() - 1
    send = lambda own, bit: lax.ppermute(own, "seq", partners(bit, bit == bits - 1, seq, seq // 4))
    got_a, got_b = [], []
    got_a.append(send(a, 0))
    half = PIECES // GROUPS
    piece = lambda k, after: nearby(kq, values, run, weights, k, PIECES, after)
    near = [piece(0, [])]
    near += [piece(k, got_a[:1]) for k in (1, 2)]
    after_a = {0: near[:1], 1: near[1:3]}
    after_b = {}
    acc, before = [None, None], [None, None]

    def add_levels(levels):
        done = []
        for g, got in enumerate((got_a, got_b)):
            source = near_of[g] if acc[g] is None else [acc[g]]
            acc[g], before[g] = distant(
                levels,
                index,
                kq,
                run,
                weights,
                source,
                [got[k] for k in levels],
                before[g],
                tok_bits,
                g * (HEADS // GROUPS),
            )
            done.append(before[g])
        return done

    for bit in range(bits):
        if bit >= 1:
            got_a.append(send(a, bit))
        if bit == 2:
            near.append(piece(3, got_a[1:2]))
            after_a[2] = near[3:]
            near_of = [near[:half], near[half:]]
        if bit >= 1:
            b = held(b, got_a[bit - 1])
            got_b.append(send(b, bit - 1))
            if bit == bits - 1:
                after_b[bit - 1] = add_levels(tuple(range(bits - 2))[2:])
            b = merge(bit - 1, index, b, got_b[bit - 1], after_b.get(bit - 1, []))
        if bit < bits - 1:
            if bit == bits - 2:
                after_a[bit] = add_levels((0, 1))
            a = merge(bit, index, a, got_a[bit], after_a.get(bit, []))
    b = held(b, got_a[bits - 1])
    got_b.append(send(b, bits - 1))
    add_levels((bits - 2,))
    column = (tok_bits + bits) * HEADS
    return acc, before, [got_a[-1], got_b[-1]], column


def body(
    activations,
    norm_gain,
    value_weight,
    shared_weight,
    rate_weight,
    rate_bias,
    decay_rate,
    level_table,
    level_ids,
    out_gain,
    out_weight,
):
    p = {
        "gain": norm_gain,
        "wv": value_weight[0],
        "ws": shared_weight[0],
        "wr": rate_weight[0].T,
        "bias": rate_bias,
        "rate": decay_rate,
    }
    index = lax.axis_index("seq").astype(jnp.int32).reshape(1)
    x = activations[0]
    rows = x.shape[0]
    values, kq, p["wr128"], p["bias128"], p["rate128"], run, a, b = project_first(x, p)
    weights = level_weights(level_ids[0], level_table[0])
    acc, before, far, column = mix(values, kq, run, a, b, index, weights)
    count = lax.axis_size("section")
    route = [(i, (i + 1) % count) for i in range(count)]
    part = rows // PARTS
    made = []
    for k in range(PARTS):
        handed = finish(
            k * part, part, 1, kq, run, weights, out_gain, x, out_weight[0], acc, before, far, column
        )
        arrived = lax.ppermute(handed, "section", route)
        made = project_next(k, rows, arrived, p, list(made))
    values, kq, ld, x = made
    run, a, b = block_state(ld, kq, values, GROUPS)
    acc, before, far, column = mix(values, kq, run, a, b, index, weights)
    result = finish(
        0, part, PARTS, kq, run, weights, out_gain, x, out_weight[0], acc, before, far, column
    )
    return result[None]


def solution(mesh):
    placed = (
        P("section", "seq", None),
        P("section", None),
        P("section", None, None),
        P("section", None, None),
        P("section", None, None),
        P("section", None),
        P("section", None),
        P("section", None, None, None),
        P("section", "seq", None),
        P("section", None),
        P("section", None, None),
    )
    return jax.shard_map(
        body, mesh=mesh, in_specs=placed, out_specs=P("section", "seq", None), check_vma=False
    )
```
